32 devices in a mesh: fam: 2 (over x), ctx: 8 (over z, y), head: 2 (over core).
Axes of the slice: x: 2, y: 2, z: 4, core: 2. Of those that a mesh axis runs over, the one named last changes fastest.
Arguments:
- prior_stream: bfloat16 [3072, 1024], P(('fam', 'ctx')), parts along dimension 0, may hold values from -6 to 6
- seq_lengths: int32 [16], P('fam'), parts along dimension 0, may hold values from 1 to 384, 1536 in all
- gain_first: float32 [1024], replicated, may hold values from 0.1 to 1.9
- qkv_first: bfloat16 [1024, 3, 1024], P(None, None, 'head'), may hold values from -1 to 1
- out_first: bfloat16 [1024, 1024], P('head'), may hold values from -0.1875 to 0.1875
- gain_second: float32 [1024], replicated, may hold values from 0.1 to 1.9
- qkv_second: bfloat16 [1024, 3, 1024], P(None, None, 'head'), may hold values from -1 to 1
- out_second: bfloat16 [1024, 1024], P('head'), may hold values from -0.1875 to 0.1875
Outputs:
- layer_output: bfloat16 [3072, 1024], P(('fam', 'ctx'), 'head'), parts along dimension 0
The draws below stay inside these ranges and needn't reach their ends.
There are 2 independent parts, one for each index of `fam`. The reference program is written for one: setup_inputs(seed, part) draws one part's arguments, and reference() takes and returns one part's arrays. A program takes and returns all parts, laid end to end along the dimension named above; an argument that names none is the same for every part. Nothing has to cross between parts.
Inputs may be any that keep to these rules, and one draw needn't show every extreme that they name: seq_lengths sum to 1536 and the largest is exactly 384.
All inputs are finite; a program needn't handle non-finite values.
Results may differ from the reference program's by a relative error of at most 0.013.
Values may be sent and summed in bfloat16 or wider, within the bound.
A program may use at most 128 MiB of HBM per device.

```python
import math
import jax
import jax.numpy as jnp
import numpy as np
from jax import lax

D = 1024
HEADS = 16
TOK_DEV = 192
LEN = 1536
NSEQ = 8
MAXLEN = 384


def projection_table(key, salt):
    folded = jax.random.fold_in(key, salt)
    parts = jax.random.split(folded, 3)
    head_dim = D // HEADS
    base = jax.random.truncated_normal(parts[0], -4.0, 4.0, (D, 3, D), jnp.float32) * D ** (-0.5)
    query_scale = jnp.exp(jax.random.uniform(parts[1], (HEADS,), jnp.float32, 0.0, math.log(3.0)))
    key_scale = jnp.exp(jax.random.uniform(parts[2], (HEADS,), jnp.float32, 0.0, math.log(3.0)))
    query_cols = jnp.repeat(query_scale, head_dim)
    key_cols = jnp.repeat(key_scale, head_dim)
    queries = base[:, 0, :] * query_cols[None, :]
    keys = base[:, 1, :] * key_cols[None, :]
    values = base[:, 2, :]
    table = jnp.stack([queries, keys, values], axis=1)
    return jnp.clip(table, -1.0, 1.0)


def draw_qkv_first(key, part):
    return projection_table(key, 11).astype(jnp.bfloat16)


def draw_qkv_second(key, part):
    return projection_table(key, 23).astype(jnp.bfloat16)


def steps_of(stream_key, extent, shards, least, top_value):
    loudness = 1.0
    for dim, blocks in shards:
        heights = jax.random.uniform(jax.random.fold_in(jax.random.fold_in(stream_key, 6), dim), (blocks,), jnp.float32, least / len(shards), top_value / len(shards))
        loudness = loudness * jnp.repeat(jnp.exp(heights), extent[dim] // blocks).reshape((-1,) + (1,) * (len(extent) - 1 - dim))
    return loudness


def profile(number_of, total, most, skew):
    portions = [(1 << 20) // math.isqrt(standing ** skew) + 1 for standing in range(2, number_of + 1)]
    spare, given = total - most - (number_of - 1), [1] * (number_of - 1)
    while spare > 0:
        candidates = [i for i in range(number_of - 1) if given[i] < most]
        mass, remaining = sum([portions[i] for i in candidates]), spare
        for i in candidates:
            extra = min(most - given[i], max(1, remaining * portions[i] // mass), spare)
            given[i] = given[i] + extra
            spare = spare - extra
    return np.array([most] + given)


def uneven_parts(key, number_of, total, limit, slope):
    if number_of == 2:
        one = jax.random.randint(key, (), max(1, total - limit), min(limit, total - 1) + 1)
        return jnp.stack([one, total - one])
    lengths = jnp.asarray(profile(number_of, total, limit, slope), jnp.int32)
    twos = (number_of - 1) // 2
    donor, receiver = lengths[1:1 + 2 * twos:2], lengths[2:2 + 2 * twos:2]
    slack = jnp.minimum(donor - 1, limit - receiver)
    moved = jax.random.randint(jax.random.fold_in(key, 1), (twos,), 0, 1 << 20) % (slack + 1)
    lengths = lengths.at[1:1 + 2 * twos:2].set(donor - moved).at[2:2 + 2 * twos:2].set(receiver + moved)
    return lengths[jax.random.permutation(jax.random.fold_in(key, 2), number_of)]


def normal_values(own_key, shape, scale, reach, cuts=(), held_as=jnp.bfloat16):
    drawn = jax.random.normal(own_key, shape, jnp.float32) * scale
    if len(cuts) > 0:
        drawn = steps_of(own_key, shape, cuts, -0.22, 0.18) * drawn
    return jnp.clip(drawn, min=-reach, max=reach).astype(held_as)


def setup_inputs(seed: int = 0, part: int = 0) -> dict:
    splits = jax.random.split(jax.random.key(seed), 9)
    own_keys = jax.random.split(jax.random.fold_in(splits[8], part), 9)
    prior_stream = normal_values(own_keys[0], (LEN, D), 1.0, 6.0, ((0, 8),))
    seq_lengths = uneven_parts(own_keys[1], NSEQ, LEN, MAXLEN, 2).astype(jnp.int32)
    gain_first = jnp.clip(1.0 + 0.18 * jax.random.normal(splits[2], (D,), jnp.float32), 0.1, 1.9)
    qkv_first = draw_qkv_first(jax.random.fold_in(splits[8], 71), part)
    out_first = normal_values(splits[4], (D, D), D ** -0.5, 0.1875, ((0, 2),))
    gain_second = jnp.clip(1.0 + 0.18 * jax.random.normal(splits[5], (D,), jnp.float32), 0.1, 1.9)
    qkv_second = draw_qkv_second(jax.random.fold_in(splits[8], 71), part)
    out_second = normal_values(splits[7], (D, D), D ** -0.5, 0.1875, ((0, 2),))
    return {"prior_stream": prior_stream, "seq_lengths": seq_lengths, "gain_first": gain_first, "qkv_first": qkv_first, "out_first": out_first, "gain_second": gain_second, "qkv_second": qkv_second, "out_second": out_second}


def rms_scaled(hidden, gain):
    values = hidden.astype(jnp.float32)
    scale = lax.rsqrt(lax.optimization_barrier(jnp.mean(values * values, axis=-1, keepdims=True)) + 1e-05)
    return (values * scale * gain.astype(jnp.float32)).astype(jnp.bfloat16)

def project_all(normed, table):
    return tuple((jnp.dot(normed, table[:, column_set, :], preferred_element_type=jnp.float32).astype(jnp.bfloat16) for column_set in range(3)))

def attend_exact(queries, keys, values, allowed):
    head_dim = D // HEADS
    query_heads = queries.astype(jnp.float32).reshape(queries.shape[0], -1, head_dim)
    key_heads = keys.astype(jnp.float32).reshape(keys.shape[0], -1, head_dim)
    value_heads = values.astype(jnp.float32).reshape(values.shape[0], -1, head_dim)
    scores = jnp.einsum('qhd,khd->hqk', query_heads, key_heads) * head_dim ** (-0.5)
    scores = jnp.where(allowed[None], scores, -jnp.inf)
    row_top = lax.optimization_barrier(jnp.max(scores, axis=-1, keepdims=True))
    exponent = jnp.where(allowed[None], jnp.exp(scores - row_top), 0.0)
    row_total = lax.optimization_barrier(jnp.sum(exponent, axis=-1))
    weights = lax.optimization_barrier(exponent.astype(jnp.bfloat16)).astype(jnp.float32)
    mixed = jnp.einsum('hqk,khd->qhd', weights, value_heads) / jnp.transpose(row_total)[:, :, None]
    return mixed.reshape(queries.shape[0], -1).astype(jnp.bfloat16)

def reference(prior_stream, seq_lengths, gain_first, qkv_first, out_first, gain_second, qkv_second, out_second):
    starts = (jnp.cumsum(seq_lengths) - seq_lengths).astype(jnp.int32)

    def segment_of(position):
        return (lax.optimization_barrier(jnp.sum((starts[None, :] <= position[:, None]).astype(jnp.int32), axis=1)) - 1).astype(jnp.int32)
    first_hidden = prior_stream
    normed_first = rms_scaled(first_hidden, gain_first)
    q_first, k_first, v_first = project_all(normed_first, qkv_first)
    margin = 2 * TOK_DEV
    pad_keys = jnp.concatenate([jnp.zeros((margin, D), k_first.dtype), k_first], axis=0)
    pad_values = jnp.concatenate([jnp.zeros((margin, D), v_first.dtype), v_first], axis=0)

    def local_block(block):
        first_row = (block * TOK_DEV).astype(jnp.int32)
        queries = lax.dynamic_slice_in_dim(q_first, first_row, TOK_DEV, 0)
        keys = lax.dynamic_slice_in_dim(pad_keys, first_row, 3 * TOK_DEV, 0)
        values = lax.dynamic_slice_in_dim(pad_values, first_row, 3 * TOK_DEV, 0)
        query_pos = first_row + jnp.arange(TOK_DEV, dtype=jnp.int32)
        key_pos = first_row - margin + jnp.arange(3 * TOK_DEV, dtype=jnp.int32)
        allowed = (key_pos[None, :] <= query_pos[:, None]) & (key_pos[None, :] >= 0)
        allowed = allowed & (segment_of(key_pos)[None, :] == segment_of(query_pos)[:, None])
        return attend_exact(queries, keys, values, allowed)
    blocks = jnp.arange(LEN // TOK_DEV, dtype=jnp.int32)
    mixed_first = lax.map(local_block, blocks).reshape(LEN, D)
    second_hidden = (first_hidden.astype(jnp.float32) + jnp.dot(mixed_first, out_first, preferred_element_type=jnp.float32)).astype(jnp.bfloat16)
    normed_second = rms_scaled(second_hidden, gain_second)
    q_second, k_second, v_second = project_all(normed_second, qkv_second)
    every_pos = jnp.arange(LEN, dtype=jnp.int32)

    def causal_block(block):
        first_row = (block * TOK_DEV).astype(jnp.int32)
        queries = lax.dynamic_slice_in_dim(q_second, first_row, TOK_DEV, 0)
        query_pos = first_row + jnp.arange(TOK_DEV, dtype=jnp.int32)
        allowed = every_pos[None, :] <= query_pos[:, None]
        return attend_exact(queries, k_second, v_second, allowed)
    mixed_second = lax.map(causal_block, blocks).reshape(LEN, D)
    return (second_hidden.astype(jnp.float32) + jnp.dot(mixed_second, out_second, preferred_element_type=jnp.float32)).astype(jnp.bfloat16)
```

```python
import functools

import jax
import jax.numpy as jnp
from jax import lax
from jax.experimental import pallas as pl
from jax.experimental.pallas import tpu as pltpu
from jax.sharding import PartitionSpec as P

HEADS = 16
MESH = pl.DeviceIdType.MESH
NEG = -1e30
BF16 = jnp.bfloat16
F32 = jnp.float32

UP, RIGHT, LEFT, SIBLING = range(4)


def fast_size(count):
    size = 1
    while (2 * size) * (2 * size) <= count:
        size *= 2
    return size


def dot(left, right):
    return jnp.dot(left, right, preferred_element_type=F32)


def rms_scaled(values, gain):
    scale = lax.rsqrt(jnp.mean(values * values, axis=-1, keepdims=True) + 1e-05)
    return (values * scale * gain).astype(BF16)


def kernel(
    count,
    fast,
    head_dim,
    prior_ref,
    lens_ref,
    gain1_ref,
    gain2_ref,
    w1_hbm,
    o1_hbm,
    w2_hbm,
    o2_hbm,
    out_ref,
    w1,
    w2,
    o1,
    o2,
    win,
    blk,
    hid,
    mix1,
    mix2,
    qs,
    top,
    acc,
    load_sem,
    win_send,
    win_recv,
    win_fwd,
    win_sib,
    wgt_send,
    wgt_recv,
    mix_send,
    mix_recv,
    blk_send,
    blk_recv,
    blk_sib,
):
    slow = count // fast
    rows = prior_ref.shape[0]
    half = w1.shape[2]
    pair_width = 2 * head_dim
    pairs = half // pair_width
    me = lax.axis_index("ctx")
    head = lax.axis_index("head")
    other = 1 - head
    a = me // fast
    b = lax.rem(me, fast)
    sibling = {"head": other}
    own_cols = pl.ds(pl.multiple_of(head * half, half), half)
    other_cols = pl.ds(pl.multiple_of(other * half, half), half)

    loads = [
        pltpu.make_async_copy(w1_hbm, w1, load_sem.at[0]),
        pltpu.make_async_copy(o1_hbm, o1.at[head], load_sem.at[1]),
        pltpu.make_async_copy(w2_hbm, w2, load_sem.at[2]),
        pltpu.make_async_copy(o2_hbm.at[:, own_cols], o2.at[head], load_sem.at[3]),
    ]
    for load in loads:
        load.start()

    barrier = pltpu.get_barrier_semaphore()
    offsets = sorted({1, 2, fast})
    for offset in offsets:
        for step in (offset, -offset):

            @pl.when((me + step >= 0) & (me + step < count))
            def _():
                pl.semaphore_signal(
                    barrier, inc=1, device_id={"ctx": me + step}, device_id_type=MESH
                )

    pl.semaphore_signal(barrier, inc=1, device_id=sibling, device_id_type=MESH)
    peers = jnp.int32(1)
    for offset in offsets:
        peers = peers + (me >= offset).astype(jnp.int32)
        peers = peers + (me + offset < count).astype(jnp.int32)
    pl.semaphore_wait(barrier, peers)

    def window_copy(distance):
        return pltpu.make_async_remote_copy(
            src_ref=prior_ref.at[:, own_cols],
            dst_ref=win.at[distance - 1, head],
            send_sem=win_send.at[distance - 1],
            recv_sem=win_recv.at[distance - 1],
            device_id={"ctx": me + distance},
            device_id_type=MESH,
        )

    def window_forward(distance, side):
        return pltpu.make_async_remote_copy(
            src_ref=win.at[distance - 1, side],
            dst_ref=win.at[distance - 1, side],
            send_sem=win_fwd.at[distance - 1],
            recv_sem=win_sib.at[distance - 1],
            device_id=sibling,
            device_id_type=MESH,
        )

    for distance in (1, 2):

        @pl.when(me + distance < count)
        def _():
            window_copy(distance).start()

    def weight_copy(index, side):
        source, target = ((o1_hbm, o1), (o2_hbm.at[:, other_cols], o2))[index]
        return pltpu.make_async_remote_copy(
            src_ref=source,
            dst_ref=target.at[side],
            send_sem=wgt_send.at[index],
            recv_sem=wgt_recv.at[index],
            device_id=sibling,
            device_id_type=MESH,
        )

    for index in (0, 1):
        weight_copy(index, head).start()

    def mix_copy(buffer, index, side):
        return pltpu.make_async_remote_copy(
            src_ref=buffer.at[side],
            dst_ref=buffer.at[side],
            send_sem=mix_send.at[index],
            recv_sem=mix_recv.at[index],
            device_id=sibling,
            device_id_type=MESH,
        )

    lane = lax.broadcasted_iota(jnp.int32, (rows, pair_width), 1)
    low_lanes = lane < head_dim
    scale = head_dim ** (-0.5)

    def set_queries(query):
        for pair in range(pairs):
            part = query[:, pair * pair_width : (pair + 1) * pair_width] * scale
            qs[pair, :rows, :] = jnp.where(low_lanes, part, 0.0).astype(BF16)
            qs[pair, rows:, :] = jnp.where(low_lanes, 0.0, part).astype(BF16)

    def attend(keys, values, allowed, first):
        ones = jnp.ones((keys.shape[0], 128), BF16)
        for pair in range(pairs):
            cols = slice(pair * pair_width, (pair + 1) * pair_width)
            scores = lax.dot_general(
                qs[pair], keys[:, cols], (((1,), (1,)), ((), ())), preferred_element_type=F32
            )
            if allowed is not None:
                scores = jnp.where(allowed, scores, NEG)
            new_top = jnp.max(scores, axis=1, keepdims=True)
            if not first:
                old_top = top[pair]
                new_top = jnp.maximum(old_top, new_top)
            weights = jnp.exp(scores - new_top)
            if allowed is not None:
                weights = jnp.where(allowed, weights, 0.0)
            added = dot(weights.astype(BF16), jnp.concatenate([values[:, cols], ones], axis=1))
            if first:
                acc[pair] = added
            else:
                acc[pair] = acc[pair] * jnp.exp(old_top - new_top) + added
            top[pair] = new_top

    def finish(buffer):
        for pair in range(pairs):
            mixed = acc[pair, :, :pair_width] / acc[pair, :, pair_width : pair_width + 1]
            mixed = jnp.where(low_lanes, mixed[:rows], mixed[rows:])
            buffer[head, :, pair * pair_width : (pair + 1) * pair_width] = mixed.astype(BF16)

    row = lax.broadcasted_iota(jnp.int32, (2 * rows, 1), 0)
    row = jnp.where(row >= rows, row - rows, row)
    query_pos = me * rows + row
    key_row = lax.broadcasted_iota(jnp.int32, (2 * rows, rows), 1)
    start_of = jnp.zeros((2 * rows, 1), jnp.int32)
    start = jnp.int32(0)
    for index in range(lens_ref.shape[0]):
        start_of = jnp.where(query_pos >= start, jnp.maximum(start_of, start), start_of)
        start = start + lens_ref[index]
    causal = key_row <= row

    gain1 = gain1_ref[...]
    normed = rms_scaled(prior_ref[...].astype(F32), gain1)
    loads[0].wait()
    set_queries(dot(normed, w1[0]).astype(BF16).astype(F32))
    attend(
        dot(normed, w1[1]).astype(BF16),
        dot(normed, w1[2]).astype(BF16),
        causal & (me * rows + key_row >= start_of),
        True,
    )
    for distance in (1, 2):

        @pl.when(me >= distance)
        def _():
            window_copy(distance).wait_recv()
            window_forward(distance, head).start()

    for distance in (1, 2):

        @pl.when(me >= distance)
        def _():
            window_forward(distance, other).wait_recv()
            hidden = jnp.concatenate([win[distance - 1, 0], win[distance - 1, 1]], axis=1)
            before = rms_scaled(hidden.astype(F32), gain1)
            attend(
                dot(before, w1[1]).astype(BF16),
                dot(before, w1[2]).astype(BF16),
                (me - distance) * rows + key_row >= start_of,
                False,
            )

    finish(mix1)
    mix_copy(mix1, 0, head).start()
    loads[1].wait()
    total = prior_ref[...].astype(F32)
    weight_copy(0, other).wait_recv()
    mix_copy(mix1, 0, other).wait_recv()
    total = total + (dot(mix1[0], o1[0]) + dot(mix1[1], o1[1]))
    second = total.astype(BF16)
    hid[0] = second[:, :half]
    hid[1] = second[:, half:]
    normed = rms_scaled(second.astype(F32), gain2_ref[...])
    blk[me, 0] = normed[:, :half]
    blk[me, 1] = normed[:, half:]

    def block_copy(block, side, place, where, recv):
        return pltpu.make_async_remote_copy(
            src_ref=blk.at[block, side],
            dst_ref=blk.at[block, side],
            send_sem=blk_send.at[block, place],
            recv_sem=recv.at[block],
            device_id=where,
            device_id_type=MESH,
        )

    def hops(block, go_up, go_right, go_left, act):
        for place, go, step in ((UP, go_up, fast), (RIGHT, go_right, 1), (LEFT, go_left, -1)):
            if go is not None:

                @pl.when(go)
                def _():
                    act(block_copy(block, head, place, {"ctx": me + step}, blk_recv))

    has_up, has_right, has_left = a + 1 < slow, b + 1 < fast, b >= 1
    hops(me, has_up, has_right, None, lambda copy: copy.start())

    def slot(stage, entry):
        away = (entry + 1) // 2
        from_left = lax.rem(entry, 2) == 1
        side = jnp.where(from_left, -away, away)
        block_a = a - stage + away
        block_b = b + side
        valid = (block_a >= 0) & (away <= stage) & (block_b >= 0) & (block_b < fast)
        valid = valid & ((away < stage) | from_left)
        return valid, block_a * fast + block_b, away == 0, from_left

    def for_slots(stage, body):
        def step(entry, carried):
            valid, block, column, from_left = slot(stage, entry)

            @pl.when(valid)
            def _():
                body(block, column, from_left)

            return carried

        lax.fori_loop(0, 2 * fast - 1, step, 0)

    def directions(column, from_left):
        go_right = has_right & (column | from_left)
        go_left = has_left & (column | jnp.logical_not(from_left))
        return has_up & column, go_right, go_left

    def pass_on(block, column, from_left):
        block_copy(block, head, UP, sibling, blk_recv).wait_recv()
        hops(block, *directions(column, from_left), lambda copy: copy.start())
        block_copy(block, head, SIBLING, sibling, blk_sib).start()

    def use(block, column, from_left):
        block_copy(block, other, SIBLING, sibling, blk_sib).wait_recv()
        source = jnp.concatenate([blk[block, 0], blk[block, 1]], axis=1)
        attend(dot(source, w2[1]).astype(BF16), dot(source, w2[2]).astype(BF16), None, False)

    def drain(block, column, from_left):
        hops(block, *directions(column, from_left), lambda copy: copy.wait_send())
        block_copy(block, head, SIBLING, sibling, blk_sib).wait_send()

    loads[2].wait()
    set_queries(dot(normed, w2[0]).astype(BF16).astype(F32))
    attend(dot(normed, w2[1]).astype(BF16), dot(normed, w2[2]).astype(BF16), causal, True)
    stages = slow + fast - 2

    def stage_step(stage, carried):
        for_slots(stage, pass_on)
        for_slots(stage - 1, use)
        return carried

    for_slots(1, pass_on)
    lax.fori_loop(2, stages + 1, stage_step, 0)
    for_slots(stages, use)

    finish(mix2)
    mix_copy(mix2, 1, head).start()
    loads[3].wait()
    weight_copy(1, other).wait_recv()
    mix_copy(mix2, 1, other).wait_recv()
    share = dot(mix2[0], o2[0]) + dot(mix2[1], o2[1])
    out_ref[...] = (hid[head].astype(F32) + share).astype(BF16)

    for distance in (1, 2):

        @pl.when(me + distance < count)
        def _():
            window_copy(distance).wait_send()

        @pl.when(me >= distance)
        def _():
            window_forward(distance, head).wait_send()

    for index in (0, 1):
        weight_copy(index, head).wait_send()
    mix_copy(mix1, 0, head).wait_send()
    mix_copy(mix2, 1, head).wait_send()
    hops(me, has_up, has_right, None, lambda copy: copy.wait_send())

    def drain_step(stage, carried):
        for_slots(stage, drain)
        return carried

    lax.fori_loop(1, stages + 1, drain_step, 0)


def per_device(
    count,
    prior_stream,
    seq_lengths,
    gain_first,
    qkv_first,
    out_first,
    gain_second,
    qkv_second,
    out_second,
):
    rows, width = prior_stream.shape
    head_dim = width // HEADS
    half = qkv_first.shape[2]
    pair_width = 2 * head_dim
    pairs = half // pair_width
    fast = fast_size(count)
    dma = pltpu.SemaphoreType.DMA
    vmem = pl.BlockSpec(memory_space=pltpu.VMEM)
    anywhere = pl.BlockSpec(memory_space=pl.ANY)
    return pl.pallas_call(
        functools.partial(kernel, count, fast, head_dim),
        out_shape=jax.ShapeDtypeStruct((rows, half), BF16),
        in_specs=[
            vmem,
            pl.BlockSpec(memory_space=pltpu.SMEM),
            vmem,
            vmem,
            anywhere,
            anywhere,
            anywhere,
            anywhere,
        ],
        out_specs=vmem,
        scratch_shapes=[
            pltpu.VMEM((3, width, half), BF16),
            pltpu.VMEM((3, width, half), BF16),
            pltpu.VMEM((2, half, width), BF16),
            pltpu.VMEM((2, half, half), BF16),
            pltpu.VMEM((2, 2, rows, half), BF16),
            pltpu.VMEM((count, 2, rows, half), BF16),
            pltpu.VMEM((2, rows, half), BF16),
            pltpu.VMEM((2, rows, half), BF16),
            pltpu.VMEM((2, rows, half), BF16),
            pltpu.VMEM((pairs, 2 * rows, pair_width), BF16),
            pltpu.VMEM((pairs, 2 * rows, 1), F32),
            pltpu.VMEM((pairs, 2 * rows, pair_width + 128), F32),
            dma((4,)),
            dma((2,)),
            dma((2,)),
            dma((2,)),
            dma((2,)),
            dma((2,)),
            dma((2,)),
            dma((2,)),
            dma((2,)),
            dma((count, 4)),
            dma((count,)),
            dma((count,)),
        ],
        compiler_params=pltpu.CompilerParams(
            collective_id=0, has_side_effects=True, vmem_limit_bytes=56 << 20
        ),
        name="tiered_layer",
    )(
        prior_stream,
        seq_lengths,
        gain_first.reshape(1, width),
        gain_second.reshape(1, width),
        jnp.transpose(qkv_first, (1, 0, 2)),
        out_first,
        jnp.transpose(qkv_second, (1, 0, 2)),
        out_second,
    )


def solution(mesh):
    in_specs = (
        P(("fam", "ctx"), None),
        P("fam"),
        P(),
        P(None, None, "head"),
        P("head", None),
        P(),
        P(None, None, "head"),
        P("head", None),
    )
    out_specs = P(("fam", "ctx"), "head")
    return jax.shard_map(
        functools.partial(per_device, mesh.shape["ctx"]),
        mesh=mesh,
        in_specs=in_specs,
        out_specs=out_specs,
        check_vma=False,
    )
```

```python
import functools

import jax
import jax.numpy as jnp
from jax import lax
from jax.experimental import pallas as pl
from jax.experimental.pallas import tpu as pltpu
from jax.sharding import PartitionSpec as P

HEADS = 16
MESH = pl.DeviceIdType.MESH
NEG = -1e30
BF16 = jnp.bfloat16
F32 = jnp.float32

UP, RIGHT, LEFT, SIBLING = range(4)


def fast_size(count):
    size = 1
    while (2 * size) * (2 * size) <= count:
        size *= 2
    return size


def dot(left, right):
    return jnp.dot(left, right, preferred_element_type=F32)


def dot_rows(left, right):
    return lax.dot_general(left, right, (((1,), (1,)), ((), ())), preferred_element_type=F32)


def rms_scaled(values, gain):
    scale = lax.rsqrt(jnp.mean(values * values, axis=-1, keepdims=True) + 1e-05)
    return (values * scale * gain).astype(BF16)


def kernel(
    count,
    fast,
    head_dim,
    prior_ref,
    lens_ref,
    gain1_ref,
    gain2_ref,
    w1_hbm,
    o1_hbm,
    w2_hbm,
    o2_hbm,
    out_ref,
    w1,
    w2,
    w1_turned,
    w2_turned,
    o1,
    o2,
    win,
    blk,
    hid,
    mix1,
    mix2,
    qs,
    top,
    sums,
    acc,
    load_sem,
    win_send,
    win_recv,
    win_fwd,
    win_sib,
    wgt_send,
    wgt_recv,
    mix_send,
    mix_recv,
    blk_send,
    blk_recv,
    blk_sib,
):
    slow = count // fast
    rows = prior_ref.shape[0]
    half = w1.shape[2]
    pair_width = 2 * head_dim
    pairs = half // pair_width
    me = lax.axis_index("ctx")
    head = lax.axis_index("head")
    other = 1 - head
    a = me // fast
    b = lax.rem(me, fast)
    sibling = {"head": other}
    own_cols = pl.ds(pl.multiple_of(head * half, half), half)
    other_cols = pl.ds(pl.multiple_of(other * half, half), half)

    loads = [
        pltpu.make_async_copy(w1_hbm, w1, load_sem.at[0]),
        pltpu.make_async_copy(o1_hbm, o1.at[head], load_sem.at[1]),
        pltpu.make_async_copy(w2_hbm, w2, load_sem.at[2]),
        pltpu.make_async_copy(o2_hbm.at[:, own_cols], o2.at[head], load_sem.at[3]),
    ]
    for load in loads:
        load.start()

    barrier = pltpu.get_barrier_semaphore()
    offsets = sorted({1, 2, fast})
    for offset in offsets:
        for step in (offset, -offset):

            @pl.when((me + step >= 0) & (me + step < count))
            def _():
                pl.semaphore_signal(
                    barrier, inc=1, device_id={"ctx": me + step}, device_id_type=MESH
                )

    pl.semaphore_signal(barrier, inc=1, device_id=sibling, device_id_type=MESH)
    peers = jnp.int32(1)
    for offset in offsets:
        peers = peers + (me >= offset).astype(jnp.int32)
        peers = peers + (me + offset < count).astype(jnp.int32)
    pl.semaphore_wait(barrier, peers)

    def window_copy(distance):
        return pltpu.make_async_remote_copy(
            src_ref=prior_ref.at[:, own_cols],
            dst_ref=win.at[distance - 1, head],
            send_sem=win_send.at[distance - 1],
            recv_sem=win_recv.at[distance - 1],
            device_id={"ctx": me + distance},
            device_id_type=MESH,
        )

    def window_forward(distance, side):
        return pltpu.make_async_remote_copy(
            src_ref=win.at[distance - 1, side],
            dst_ref=win.at[distance - 1, side],
            send_sem=win_fwd.at[distance - 1],
            recv_sem=win_sib.at[distance - 1],
            device_id=sibling,
            device_id_type=MESH,
        )

    for distance in (1, 2):

        @pl.when(me + distance < count)
        def _():
            window_copy(distance).start()

    def weight_copy(index, side):
        source, target = ((o1_hbm, o1), (o2_hbm.at[:, other_cols], o2))[index]
        return pltpu.make_async_remote_copy(
            src_ref=source,
            dst_ref=target.at[side],
            send_sem=wgt_send.at[index],
            recv_sem=wgt_recv.at[index],
            device_id=sibling,
            device_id_type=MESH,
        )

    for index in (0, 1):
        weight_copy(index, head).start()

    def mix_copy(buffer, index, side):
        return pltpu.make_async_remote_copy(
            src_ref=buffer.at[side],
            dst_ref=buffer.at[side],
            send_sem=mix_send.at[index],
            recv_sem=mix_recv.at[index],
            device_id=sibling,
            device_id_type=MESH,
        )

    lane = lax.broadcasted_iota(jnp.int32, (rows, pair_width), 1)
    low_lanes = lane < head_dim
    scale = head_dim ** (-0.5)

    def set_queries(query):
        for pair in range(pairs):
            part = query[:, pair * pair_width : (pair + 1) * pair_width] * scale
            qs[pair, :rows, :] = jnp.where(low_lanes, part, 0.0).astype(BF16)
            qs[pair, rows:, :] = jnp.where(low_lanes, 0.0, part).astype(BF16)

    def project(source, table, turned):
        keys = dot(source, table[1]).astype(BF16)
        return keys, dot_rows(turned[...], source).astype(BF16)

    def attend(keys, values, allowed, first):
        for pair in range(pairs):
            cols = slice(pair * pair_width, (pair + 1) * pair_width)
            scores = dot_rows(keys[:, cols], qs[pair])
            if allowed is not None:
                scores = jnp.where(allowed, scores, NEG)
            new_top = jnp.max(scores, axis=0, keepdims=True)
            if not first:
                old_top = top[pair]
                new_top = jnp.maximum(old_top, new_top)
            weights = jnp.exp(scores - new_top)
            if allowed is not None:
                weights = jnp.where(allowed, weights, 0.0)
            added = dot(values[cols, :], weights.astype(BF16))
            added_sum = jnp.sum(weights, axis=0, keepdims=True)
            if first:
                acc[pair] = added
                sums[pair] = added_sum
            else:
                factor = jnp.exp(old_top - new_top)
                acc[pair] = acc[pair] * factor + added
                sums[pair] = sums[pair] * factor + added_sum
            top[pair] = new_top

    def finish(buffer):
        for pair in range(pairs):
            mixed = jnp.transpose(acc[pair] / sums[pair])
            mixed = jnp.where(low_lanes, mixed[:rows], mixed[rows:])
            buffer[head, :, pair * pair_width : (pair + 1) * pair_width] = mixed.astype(BF16)

    row = lax.broadcasted_iota(jnp.int32, (1, 2 * rows), 1)
    row = jnp.where(row >= rows, row - rows, row)
    query_pos = me * rows + row
    key_row = lax.broadcasted_iota(jnp.int32, (rows, 2 * rows), 0)
    start_of = jnp.zeros((1, 2 * rows), jnp.int32)
    start = jnp.int32(0)
    for index in range(lens_ref.shape[0]):
        start_of = jnp.where(query_pos >= start, jnp.maximum(start_of, start), start_of)
        start = start + lens_ref[index]
    causal = key_row <= row

    gain1 = gain1_ref[...]
    normed = rms_scaled(prior_ref[...].astype(F32), gain1)
    loads[0].wait()
    set_queries(dot(normed, w1[0]).astype(BF16).astype(F32))
    w1_turned[...] = jnp.transpose(w1[2])
    attend(
        *project(normed, w1, w1_turned),
        causal & (me * rows + key_row >= start_of),
        True,
    )
    loads[2].wait()
    w2_turned[...] = jnp.transpose(w2[2])
    for distance in (1, 2):

        @pl.when(me >= distance)
        def _():
            window_copy(distance).wait_recv()
            window_forward(distance, head).start()

    for distance in (1, 2):

        @pl.when(me >= distance)
        def _():
            window_forward(distance, other).wait_recv()
            hidden = jnp.concatenate([win[distance - 1, 0], win[distance - 1, 1]], axis=1)
            before = rms_scaled(hidden.astype(F32), gain1)
            attend(
                *project(before, w1, w1_turned),
                (me - distance) * rows + key_row >= start_of,
                False,
            )

    finish(mix1)
    mix_copy(mix1, 0, head).start()
    loads[1].wait()
    total = prior_ref[...].astype(F32)
    weight_copy(0, other).wait_recv()
    mix_copy(mix1, 0, other).wait_recv()
    total = total + (dot(mix1[0], o1[0]) + dot(mix1[1], o1[1]))
    second = total.astype(BF16)
    hid[0] = second[:, :half]
    hid[1] = second[:, half:]
    normed = rms_scaled(second.astype(F32), gain2_ref[...])
    blk[me, 0] = normed[:, :half]
    blk[me, 1] = normed[:, half:]

    def block_copy(block, side, place, where, recv):
        return pltpu.make_async_remote_copy(
            src_ref=blk.at[block, side],
            dst_ref=blk.at[block, side],
            send_sem=blk_send.at[block, place],
            recv_sem=recv.at[block],
            device_id=where,
            device_id_type=MESH,
        )

    def hops(block, go_up, go_right, go_left, act):
        for place, go, step in ((UP, go_up, fast), (RIGHT, go_right, 1), (LEFT, go_left, -1)):
            if go is not None:

                @pl.when(go)
                def _():
                    act(block_copy(block, head, place, {"ctx": me + step}, blk_recv))

    has_up, has_right, has_left = a + 1 < slow, b + 1 < fast, b >= 1
    hops(me, has_up, has_right, None, lambda copy: copy.start())

    def slot(stage, entry):
        away = (entry + 1) // 2
        from_left = lax.rem(entry, 2) == 1
        side = jnp.where(from_left, -away, away)
        block_a = a - stage + away
        block_b = b + side
        valid = (block_a >= 0) & (away <= stage) & (block_b >= 0) & (block_b < fast)
        valid = valid & ((away < stage) | from_left)
        return valid, block_a * fast + block_b, away == 0, from_left

    def for_slots(stage, body):
        def step(entry, carried):
            valid, block, column, from_left = slot(stage, entry)

            @pl.when(valid)
            def _():
                body(block, column, from_left)

            return carried

        lax.fori_loop(0, 2 * fast - 1, step, 0)

    def directions(column, from_left):
        go_right = has_right & (column | from_left)
        go_left = has_left & (column | jnp.logical_not(from_left))
        return has_up & column, go_right, go_left

    def pass_on(block, column, from_left):
        block_copy(block, head, UP, sibling, blk_recv).wait_recv()
        hops(block, *directions(column, from_left), lambda copy: copy.start())
        block_copy(block, head, SIBLING, sibling, blk_sib).start()

    def use(block, column, from_left):
        block_copy(block, other, SIBLING, sibling, blk_sib).wait_recv()
        source = jnp.concatenate([blk[block, 0], blk[block, 1]], axis=1)
        attend(*project(source, w2, w2_turned), None, False)

    def drain(block, column, from_left):
        hops(block, *directions(column, from_left), lambda copy: copy.wait_send())
        block_copy(block, head, SIBLING, sibling, blk_sib).wait_send()

    set_queries(dot(normed, w2[0]).astype(BF16).astype(F32))
    attend(*project(normed, w2, w2_turned), causal, True)
    stages = slow + fast - 2

    def stage_step(stage, carried):
        for_slots(stage, pass_on)
        for_slots(stage, use)
        return carried

    lax.fori_loop(1, stages + 1, stage_step, 0)

    finish(mix2)
    mix_copy(mix2, 1, head).start()
    loads[3].wait()
    weight_copy(1, other).wait_recv()
    mix_copy(mix2, 1, other).wait_recv()
    share = dot(mix2[0], o2[0]) + dot(mix2[1], o2[1])
    out_ref[...] = (hid[head].astype(F32) + share).astype(BF16)

    for distance in (1, 2):

        @pl.when(me + distance < count)
        def _():
            window_copy(distance).wait_send()

        @pl.when(me >= distance)
        def _():
            window_forward(distance, head).wait_send()

    for index in (0, 1):
        weight_copy(index, head).wait_send()
    mix_copy(mix1, 0, head).wait_send()
    mix_copy(mix2, 1, head).wait_send()
    hops(me, has_up, has_right, None, lambda copy: copy.wait_send())

    def drain_step(stage, carried):
        for_slots(stage, drain)
        return carried

    lax.fori_loop(1, stages + 1, drain_step, 0)


def per_device(
    count,
    prior_stream,
    seq_lengths,
    gain_first,
    qkv_first,
    out_first,
    gain_second,
    qkv_second,
    out_second,
):
    rows, width = prior_stream.shape
    head_dim = width // HEADS
    half = qkv_first.shape[2]
    pair_width = 2 * head_dim
    pairs = half // pair_width
    fast = fast_size(count)
    dma = pltpu.SemaphoreType.DMA
    vmem = pl.BlockSpec(memory_space=pltpu.VMEM)
    anywhere = pl.BlockSpec(memory_space=pl.ANY)
    return pl.pallas_call(
        functools.partial(kernel, count, fast, head_dim),
        out_shape=jax.ShapeDtypeStruct((rows, half), BF16),
        in_specs=[
            vmem,
            pl.BlockSpec(memory_space=pltpu.SMEM),
            vmem,
            vmem,
            anywhere,
            anywhere,
            anywhere,
            anywhere,
        ],
        out_specs=vmem,
        scratch_shapes=[
            pltpu.VMEM((3, width, half), BF16),
            pltpu.VMEM((3, width, half), BF16),
            pltpu.VMEM((half, width), BF16),
            pltpu.VMEM((half, width), BF16),
            pltpu.VMEM((2, half, width), BF16),
            pltpu.VMEM((2, half, half), BF16),
            pltpu.VMEM((2, 2, rows, half), BF16),
            pltpu.VMEM((count, 2, rows, half), BF16),
            pltpu.VMEM((2, rows, half), BF16),
            pltpu.VMEM((2, rows, half), BF16),
            pltpu.VMEM((2, rows, half), BF16),
            pltpu.VMEM((pairs, 2 * rows, pair_width), BF16),
            pltpu.VMEM((pairs, 1, 2 * rows), F32),
            pltpu.VMEM((pairs, 1, 2 * rows), F32),
            pltpu.VMEM((pairs, pair_width, 2 * rows), F32),
            dma((4,)),
            dma((2,)),
            dma((2,)),
            dma((2,)),
            dma((2,)),
            dma((2,)),
            dma((2,)),
            dma((2,)),
            dma((2,)),
            dma((count, 4)),
            dma((count,)),
            dma((count,)),
        ],
        compiler_params=pltpu.CompilerParams(
            collective_id=0, has_side_effects=True, vmem_limit_bytes=56 << 20
        ),
        name="tiered_layer",
    )(
        prior_stream,
        seq_lengths,
        gain_first.reshape(1, width),
        gain_second.reshape(1, width),
        jnp.transpose(qkv_first, (1, 0, 2)),
        out_first,
        jnp.transpose(qkv_second, (1, 0, 2)),
        out_second,
    )


def solution(mesh):
    in_specs = (
        P(("fam", "ctx"), None),
        P("fam"),
        P(),
        P(None, None, "head"),
        P("head", None),
        P(),
        P(None, None, "head"),
        P("head", None),
    )
    out_specs = P(("fam", "ctx"), "head")
    return jax.shard_map(
        functools.partial(per_device, mesh.shape["ctx"]),
        mesh=mesh,
        in_specs=in_specs,
        out_specs=out_specs,
        check_vma=False,
    )
```

```python
import functools

import jax
import jax.numpy as jnp
from jax import lax
from jax.experimental import pallas as pl
from jax.experimental.pallas import tpu as pltpu
from jax.sharding import PartitionSpec as P

HEADS = 16
MESH = pl.DeviceIdType.MESH
NEG = -1e30
BF16 = jnp.bfloat16
F32 = jnp.float32

UP, RIGHT, LEFT, SIBLING = range(4)
PIECES = 2


def fast_size(count):
    size = 1
    while (2 * size) * (2 * size) <= count:
        size *= 2
    return size


def dot(left, right):
    return jnp.dot(left, right, preferred_element_type=F32)


def dot_rows(left, right):
    return lax.dot_general(left, right, (((1,), (1,)), ((), ())), preferred_element_type=F32)


def rms_scaled(values, gain):
    scale = lax.rsqrt(jnp.mean(values * values, axis=-1, keepdims=True) + 1e-05)
    return (values * scale * gain).astype(BF16)


def kernel(
    count,
    fast,
    head_dim,
    prior_ref,
    lens_ref,
    gain1_ref,
    gain2_ref,
    w1_hbm,
    o1_hbm,
    w2_hbm,
    o2_hbm,
    out_ref,
    w1,
    w2,
    w1_turned,
    w2_turned,
    o1,
    o2,
    win,
    blk,
    hid,
    mix1,
    mix2,
    qs,
    top,
    sums,
    acc,
    load_sem,
    win_send,
    win_recv,
    win_fwd,
    win_sib,
    wgt_send,
    wgt_recv,
    mix_send,
    mix_recv,
    blk_send,
    blk_recv,
    blk_sib,
):
    slow = count // fast
    rows = prior_ref.shape[0]
    half = w1.shape[2]
    pair_width = 2 * head_dim
    pairs = half // pair_width
    me = lax.axis_index("ctx")
    head = lax.axis_index("head")
    other = 1 - head
    a = me // fast
    b = lax.rem(me, fast)
    sibling = {"head": other}
    own_cols = pl.ds(pl.multiple_of(head * half, half), half)
    other_cols = pl.ds(pl.multiple_of(other * half, half), half)

    loads = [
        pltpu.make_async_copy(w1_hbm, w1, load_sem.at[0]),
        pltpu.make_async_copy(o1_hbm, o1.at[head], load_sem.at[1]),
        pltpu.make_async_copy(w2_hbm, w2, load_sem.at[2]),
        pltpu.make_async_copy(o2_hbm.at[:, own_cols], o2.at[head], load_sem.at[3]),
    ]
    for load in loads:
        load.start()

    barrier = pltpu.get_barrier_semaphore()
    offsets = sorted({1, 2, fast})
    for offset in offsets:
        for step in (offset, -offset):

            @pl.when((me + step >= 0) & (me + step < count))
            def _():
                pl.semaphore_signal(
                    barrier, inc=1, device_id={"ctx": me + step}, device_id_type=MESH
                )

    pl.semaphore_signal(barrier, inc=1, device_id=sibling, device_id_type=MESH)
    peers = jnp.int32(1)
    for offset in offsets:
        peers = peers + (me >= offset).astype(jnp.int32)
        peers = peers + (me + offset < count).astype(jnp.int32)
    pl.semaphore_wait(barrier, peers)

    def window_copy(distance):
        return pltpu.make_async_remote_copy(
            src_ref=prior_ref.at[:, own_cols],
            dst_ref=win.at[distance - 1, head],
            send_sem=win_send.at[distance - 1],
            recv_sem=win_recv.at[distance - 1],
            device_id={"ctx": me + distance},
            device_id_type=MESH,
        )

    def window_forward(distance, side):
        return pltpu.make_async_remote_copy(
            src_ref=win.at[distance - 1, side],
            dst_ref=win.at[distance - 1, side],
            send_sem=win_fwd.at[distance - 1],
            recv_sem=win_sib.at[distance - 1],
            device_id=sibling,
            device_id_type=MESH,
        )

    for distance in (1, 2):

        @pl.when(me + distance < count)
        def _():
            window_copy(distance).start()

    def weight_copy(index, side):
        source, target = ((o1_hbm, o1), (o2_hbm.at[:, other_cols], o2))[index]
        return pltpu.make_async_remote_copy(
            src_ref=source,
            dst_ref=target.at[side],
            send_sem=wgt_send.at[index],
            recv_sem=wgt_recv.at[index],
            device_id=sibling,
            device_id_type=MESH,
        )

    for index in (0, 1):
        weight_copy(index, head).start()

    def mix_copy(buffer, index, side):
        return pltpu.make_async_remote_copy(
            src_ref=buffer.at[side],
            dst_ref=buffer.at[side],
            send_sem=mix_send.at[index],
            recv_sem=mix_recv.at[index],
            device_id=sibling,
            device_id_type=MESH,
        )

    lane = lax.broadcasted_iota(jnp.int32, (rows, pair_width), 1)
    low_lanes = lane < head_dim
    scale = head_dim ** (-0.5)

    def set_queries(query):
        for pair in range(pairs):
            part = query[:, pair * pair_width : (pair + 1) * pair_width] * scale
            qs[pair, :rows, :] = jnp.where(low_lanes, part, 0.0).astype(BF16)
            qs[pair, rows:, :] = jnp.where(low_lanes, 0.0, part).astype(BF16)

    def project(source, table, turned):
        keys = dot(source, table[1]).astype(BF16)
        return keys, dot_rows(turned[...], source).astype(BF16)

    def attend(keys, values, allowed, first):
        for pair in range(pairs):
            cols = slice(pair * pair_width, (pair + 1) * pair_width)
            scores = dot_rows(keys[:, cols], qs[pair])
            if allowed is not None:
                scores = jnp.where(allowed, scores, NEG)
            new_top = jnp.max(scores, axis=0, keepdims=True)
            if not first:
                old_top = top[pair]
                new_top = jnp.maximum(old_top, new_top)
            weights = jnp.exp(scores - new_top)
            if allowed is not None:
                weights = jnp.where(allowed, weights, 0.0)
            added = dot(values[cols, :], weights.astype(BF16))
            added_sum = jnp.sum(weights, axis=0, keepdims=True)
            if first:
                acc[pair] = added
                sums[pair] = added_sum
            else:
                factor = jnp.exp(old_top - new_top)
                acc[pair] = acc[pair] * factor + added
                sums[pair] = sums[pair] * factor + added_sum
            top[pair] = new_top

    def finish(buffer):
        for pair in range(pairs):
            mixed = jnp.transpose(acc[pair] / sums[pair])
            mixed = jnp.where(low_lanes, mixed[:rows], mixed[rows:])
            buffer[head, :, pair * pair_width : (pair + 1) * pair_width] = mixed.astype(BF16)

    row = lax.broadcasted_iota(jnp.int32, (1, 2 * rows), 1)
    row = jnp.where(row >= rows, row - rows, row)
    query_pos = me * rows + row
    key_row = lax.broadcasted_iota(jnp.int32, (rows, 2 * rows), 0)
    start_of = jnp.zeros((1, 2 * rows), jnp.int32)
    start = jnp.int32(0)
    for index in range(lens_ref.shape[0]):
        start_of = jnp.where(query_pos >= start, jnp.maximum(start_of, start), start_of)
        start = start + lens_ref[index]
    causal = key_row <= row

    gain1 = gain1_ref[...]
    normed = rms_scaled(prior_ref[...].astype(F32), gain1)
    loads[0].wait()
    set_queries(dot(normed, w1[0]).astype(BF16).astype(F32))
    w1_turned[...] = jnp.transpose(w1[2])
    attend(
        *project(normed, w1, w1_turned),
        causal & (me * rows + key_row >= start_of),
        True,
    )
    loads[2].wait()
    w2_turned[...] = jnp.transpose(w2[2])
    for distance in (1, 2):

        @pl.when(me >= distance)
        def _():
            window_copy(distance).wait_recv()
            window_forward(distance, head).start()

    for distance in (1, 2):

        @pl.when(me >= distance)
        def _():
            window_forward(distance, other).wait_recv()
            hidden = jnp.concatenate([win[distance - 1, 0], win[distance - 1, 1]], axis=1)
            before = rms_scaled(hidden.astype(F32), gain1)
            attend(
                *project(before, w1, w1_turned),
                (me - distance) * rows + key_row >= start_of,
                False,
            )

    finish(mix1)
    mix_copy(mix1, 0, head).start()
    loads[1].wait()
    total = prior_ref[...].astype(F32)
    weight_copy(0, other).wait_recv()
    mix_copy(mix1, 0, other).wait_recv()
    total = total + (dot(mix1[0], o1[0]) + dot(mix1[1], o1[1]))
    second = total.astype(BF16)
    hid[0] = second[:, :half]
    hid[1] = second[:, half:]
    normed = rms_scaled(second.astype(F32), gain2_ref[...])
    blk[me, 0] = normed[:, :half]
    blk[me, 1] = normed[:, half:]

    def block_copy(block, piece, side, place, where, recv):
        part = blk.at[block, side, pl.ds(piece * (rows // PIECES), rows // PIECES)]
        return pltpu.make_async_remote_copy(
            src_ref=part,
            dst_ref=part,
            send_sem=blk_send.at[block, place, piece],
            recv_sem=recv.at[block, piece],
            device_id=where,
            device_id_type=MESH,
        )

    def hops(block, piece, go_up, go_right, go_left, act):
        for place, go, step in ((UP, go_up, fast), (RIGHT, go_right, 1), (LEFT, go_left, -1)):
            if go is not None:

                @pl.when(go)
                def _():
                    act(block_copy(block, piece, head, place, {"ctx": me + step}, blk_recv))

    has_up, has_right, has_left = a + 1 < slow, b + 1 < fast, b >= 1
    for piece in range(PIECES):
        hops(me, piece, has_up, has_right, None, lambda copy: copy.start())

    def slot(stage, entry):
        away = (entry + 1) // 2
        from_left = lax.rem(entry, 2) == 1
        side = jnp.where(from_left, -away, away)
        block_a = a - stage + away
        block_b = b + side
        valid = (block_a >= 0) & (away <= stage) & (block_b >= 0) & (block_b < fast)
        valid = valid & ((away < stage) | from_left)
        return valid, block_a * fast + block_b, away == 0, from_left

    def for_slots(stage, body):
        def step(entry, carried):
            valid, block, column, from_left = slot(stage, entry)

            @pl.when(valid)
            def _():
                body(block, column, from_left)

            return carried

        lax.fori_loop(0, 2 * fast - 1, step, 0)

    def directions(column, from_left):
        go_right = has_right & (column | from_left)
        go_left = has_left & (column | jnp.logical_not(from_left))
        return has_up & column, go_right, go_left

    def pass_on(block, column, from_left):
        for piece in range(PIECES):
            block_copy(block, piece, head, UP, sibling, blk_recv).wait_recv()
            hops(block, piece, *directions(column, from_left), lambda copy: copy.start())
            block_copy(block, piece, head, SIBLING, sibling, blk_sib).start()

    def use(block, column, from_left):
        for piece in range(PIECES):
            block_copy(block, piece, other, SIBLING, sibling, blk_sib).wait_recv()
        source = jnp.concatenate([blk[block, 0], blk[block, 1]], axis=1)
        attend(*project(source, w2, w2_turned), None, False)

    def drain(block, column, from_left):
        for piece in range(PIECES):
            hops(block, piece, *directions(column, from_left), lambda copy: copy.wait_send())
            block_copy(block, piece, head, SIBLING, sibling, blk_sib).wait_send()

    set_queries(dot(normed, w2[0]).astype(BF16).astype(F32))
    attend(*project(normed, w2, w2_turned), causal, True)
    stages = slow + fast - 2

    def stage_step(stage, carried):
        for_slots(stage, pass_on)
        for_slots(stage - lag, use)
        return carried

    lag = has_up.astype(jnp.int32)
    lax.fori_loop(1, stages + 2, stage_step, 0)

    finish(mix2)
    mix_copy(mix2, 1, head).start()
    loads[3].wait()
    weight_copy(1, other).wait_recv()
    mix_copy(mix2, 1, other).wait_recv()
    share = dot(mix2[0], o2[0]) + dot(mix2[1], o2[1])
    out_ref[...] = (hid[head].astype(F32) + share).astype(BF16)

    for distance in (1, 2):

        @pl.when(me + distance < count)
        def _():
            window_copy(distance).wait_send()

        @pl.when(me >= distance)
        def _():
            window_forward(distance, head).wait_send()

    for index in (0, 1):
        weight_copy(index, head).wait_send()
    mix_copy(mix1, 0, head).wait_send()
    mix_copy(mix2, 1, head).wait_send()
    for piece in range(PIECES):
        hops(me, piece, has_up, has_right, None, lambda copy: copy.wait_send())

    def drain_step(stage, carried):
        for_slots(stage, drain)
        return carried

    lax.fori_loop(1, stages + 1, drain_step, 0)


def per_device(
    count,
    prior_stream,
    seq_lengths,
    gain_first,
    qkv_first,
    out_first,
    gain_second,
    qkv_second,
    out_second,
):
    rows, width = prior_stream.shape
    head_dim = width // HEADS
    half = qkv_first.shape[2]
    pair_width = 2 * head_dim
    pairs = half // pair_width
    fast = fast_size(count)
    dma = pltpu.SemaphoreType.DMA
    vmem = pl.BlockSpec(memory_space=pltpu.VMEM)
    anywhere = pl.BlockSpec(memory_space=pl.ANY)
    return pl.pallas_call(
        functools.partial(kernel, count, fast, head_dim),
        out_shape=jax.ShapeDtypeStruct((rows, half), BF16),
        in_specs=[
            vmem,
            pl.BlockSpec(memory_space=pltpu.SMEM),
            vmem,
            vmem,
            anywhere,
            anywhere,
            anywhere,
            anywhere,
        ],
        out_specs=vmem,
        scratch_shapes=[
            pltpu.VMEM((3, width, half), BF16),
            pltpu.VMEM((3, width, half), BF16),
            pltpu.VMEM((half, width), BF16),
            pltpu.VMEM((half, width), BF16),
            pltpu.VMEM((2, half, width), BF16),
            pltpu.VMEM((2, half, half), BF16),
            pltpu.VMEM((2, 2, rows, half), BF16),
            pltpu.VMEM((count, 2, rows, half), BF16),
            pltpu.VMEM((2, rows, half), BF16),
            pltpu.VMEM((2, rows, half), BF16),
            pltpu.VMEM((2, rows, half), BF16),
            pltpu.VMEM((pairs, 2 * rows, pair_width), BF16),
            pltpu.VMEM((pairs, 1, 2 * rows), F32),
            pltpu.VMEM((pairs, 1, 2 * rows), F32),
            pltpu.VMEM((pairs, pair_width, 2 * rows), F32),
            dma((4,)),
            dma((2,)),
            dma((2,)),
            dma((2,)),
            dma((2,)),
            dma((2,)),
            dma((2,)),
            dma((2,)),
            dma((2,)),
            dma((count, 4, PIECES)),
            dma((count, PIECES)),
            dma((count, PIECES)),
        ],
        compiler_params=pltpu.CompilerParams(
            collective_id=0, has_side_effects=True, vmem_limit_bytes=56 << 20
        ),
        name="tiered_layer",
    )(
        prior_stream,
        seq_lengths,
        gain_first.reshape(1, width),
        gain_second.reshape(1, width),
        jnp.transpose(qkv_first, (1, 0, 2)),
        out_first,
        jnp.transpose(qkv_second, (1, 0, 2)),
        out_second,
    )


def solution(mesh):
    in_specs = (
        P(("fam", "ctx"), None),
        P("fam"),
        P(),
        P(None, None, "head"),
        P("head", None),
        P(),
        P(None, None, "head"),
        P("head", None),
    )
    out_specs = P(("fam", "ctx"), "head")
    return jax.shard_map(
        functools.partial(per_device, mesh.shape["ctx"]),
        mesh=mesh,
        in_specs=in_specs,
        out_specs=out_specs,
        check_vma=False,
    )
```
